32 devices in a mesh: dp: 16 (over z, y, x), tensor: 2 (over core).
Axes of the slice: x: 2, y: 2, z: 4, core: 2. Of those that a mesh axis runs over, the one named last changes fastest.
Arguments:
- acts: bfloat16 [1, 6144, 28672], P(None, 'dp', 'tensor'), may hold values from -6 to 6
- out_grads: bfloat16 [1, 6144, 8192], P(None, 'dp', 'tensor'), may hold values from -6 to 6
- proj_in: bfloat16 [1, 28672, 64], P(None, 'tensor'), may hold values from -0.03125 to 0.03125
- proj_out: bfloat16 [1, 8192, 64], P(None, 'tensor'), may hold values from -0.0625 to 0.0625
- doc_starts: int32 [64], P('dp'), may hold values from 0 to 191, as said below
- token_counts: int32 [16], P('dp'), may hold values from 192 to 384, as said below
- queries: float32 [256, 1, 4096], P('dp', None, 'tensor'), may hold values from -0.046875 to 0.046875
Outputs:
- scores: float32 [256, 64], P(None, 'dp')
- doc_grads: float32 [64, 1, 4096], P('dp', None, 'tensor')
The draws below stay inside these ranges and needn't reach their ends.
Inputs may be any that keep to these rules, and one draw needn't show every extreme that they name: `doc_starts`: within each block of 4 entries the first is 0, the entries rise strictly, and the last is 191. `token_counts`: entry 0 equals 384.
All inputs are finite; a program needn't handle non-finite values.
Results may differ from the reference program's by a relative error of at most 0.0003.
Values sent between devices are 32-bit elements; how exact they have to be, the bound alone decides.
A program may use at most 64 MiB of HBM per device.

```python
import jax
import jax.numpy as jnp
from jax import lax

D = 8192
FF = 28672
RANK = 64
LAYERS = 1
TOK_DEV = 384
DOCS_DEV = 4
TOKENS = 6144
DOCS = 64
QUERIES = 256
N_DP = 16


def draw_doc_starts(key, part):
    blocks = DOCS // DOCS_DEV

    def single(sub):
        order = jax.random.permutation(sub, TOK_DEV // 2 - 2) + 1
        picked = jnp.sort(order[:DOCS_DEV - 2]).astype(jnp.int32)
        head = jnp.zeros((1,), jnp.int32)
        tail = jnp.full((1,), TOK_DEV // 2 - 1, jnp.int32)
        return jnp.concatenate([head, picked, tail])
    keys = jax.random.split(jax.random.fold_in(key, 11), blocks)
    return jax.vmap(single)(keys).reshape(DOCS)


def draw_token_counts(key, part):
    blocks = DOCS // DOCS_DEV
    counts = jax.random.randint(jax.random.fold_in(key, 23), (blocks,), TOK_DEV // 2, TOK_DEV + 1).astype(jnp.int32)
    return counts.at[0].set(TOK_DEV)


def shard_levels(key, dims, pieces, low, largest):
    def one(position, blocks):
        steps = jax.random.uniform(jax.random.fold_in(jax.random.fold_in(key, 6), position), (blocks,), jnp.float32, low / len(pieces), largest / len(pieces))
        return jnp.repeat(jnp.exp(steps), dims[position] // blocks).reshape((-1,) + (1,) * (len(dims) - position - 1))

    level = one(*pieces[0])
    for cut in pieces[1:]:
        level = level * one(*cut)
    return level


def centred(rng, dims, deviation, most, shards=(), kind=jnp.bfloat16):
    drawn = deviation * jax.random.normal(rng, dims, jnp.float32)
    if shards:
        drawn = drawn * shard_levels(rng, dims, shards, -0.22, 0.18)
    return jnp.clip(drawn, -most, most).astype(kind)


def setup_inputs(seed: int = 0) -> dict:
    streams_of = jax.random.split(jax.random.key(seed), 8)
    acts = centred(streams_of[0], (LAYERS, TOKENS, FF), 1.0, 6.0, ((1, 16), (2, 2)))
    out_grads = centred(streams_of[1], (LAYERS, TOKENS, D), 1.0, 6.0, ((1, 16), (2, 2)))
    proj_in = centred(streams_of[2], (LAYERS, FF, RANK), FF ** -0.5, 0.03125, ((1, 2),))
    proj_out = centred(streams_of[3], (LAYERS, D, RANK), D ** -0.5, 0.0625, ((1, 2),))
    doc_starts = draw_doc_starts(jax.random.fold_in(streams_of[7], 71), 0)
    token_counts = draw_token_counts(jax.random.fold_in(streams_of[7], 71), 0)
    queries = centred(streams_of[6], (QUERIES, LAYERS, RANK * RANK), (RANK * RANK * LAYERS * 4) ** -0.5, 0.046875, ((0, 16), (2, 2)), jnp.float32)
    return dict(acts=acts, out_grads=out_grads, proj_in=proj_in, proj_out=proj_out, doc_starts=doc_starts, token_counts=token_counts, queries=queries)


def reference(acts, out_grads, proj_in, proj_out, doc_starts, token_counts, queries):
    left = jnp.stack([jnp.dot(acts[i], proj_in[i], preferred_element_type=jnp.float32) for i in range(LAYERS)])
    right = jnp.stack([jnp.dot(out_grads[i], proj_out[i], preferred_element_type=jnp.float32) for i in range(LAYERS)])
    starts = doc_starts.reshape(N_DP, DOCS_DEV)
    positions = jnp.arange(TOK_DEV, dtype=jnp.int32)
    doc_index = jnp.sum((positions[None, :, None] >= starts[:, None, :]).astype(jnp.int32), axis=2) - 1
    valid = positions[None, :] < token_counts[:, None]
    member = ((doc_index[:, :, None] == jnp.arange(DOCS_DEV, dtype=jnp.int32)[None, None, :]) & valid[:, :, None]).astype(jnp.float32)
    left = left.reshape(LAYERS, N_DP, TOK_DEV, RANK)
    right = right.reshape(LAYERS, N_DP, TOK_DEV, RANK)
    spread = member[None, :, :, :, None] * left[:, :, :, None, :]
    grads = jnp.einsum('lptdr,lpts->pdlrs', spread, right, precision=lax.Precision.HIGHEST)
    doc_grads = grads.reshape(DOCS, LAYERS, RANK * RANK)
    scores = jnp.dot(queries.reshape(QUERIES, LAYERS * RANK * RANK), doc_grads.reshape(DOCS, LAYERS * RANK * RANK).T, precision=lax.Precision.HIGHEST, preferred_element_type=jnp.float32)
    return scores, doc_grads
```

```python
import functools
import math

import jax
import jax.numpy as jnp
from jax import lax
from jax.experimental import pallas as pl
from jax.experimental.pallas import tpu as pltpu
from jax.sharding import PartitionSpec as P

MESH = pl.DeviceIdType.MESH
HIGHEST = lax.Precision.HIGHEST
NT = (((1,), (1,)), ((), ()))
DOC_DIMS = (True, False, False)


class Group:
    def __init__(self, n_dp):
        plane = math.gcd(n_dp, 4)
        y = math.gcd(plane, 2)
        self.sizes = (n_dp // plane, plane // y, y)
        self.nd = math.prod(s for s, m in zip(self.sizes, DOC_DIMS) if m)
        self.nq = math.prod(s for s, m in zip(self.sizes, DOC_DIMS) if not m)

    def split(self, dp):
        z = lax.div(dp, self.sizes[1] * self.sizes[2])
        y = lax.rem(lax.div(dp, self.sizes[2]), self.sizes[1])
        x = lax.rem(dp, self.sizes[2])
        doc, query = 0, 0
        for c, s, m in zip((z, y, x), self.sizes, DOC_DIMS):
            if m:
                doc = doc * s + c
            else:
                query = query * s + c
        return doc, query

    def join(self, doc, query):
        div = (lambda a, b: a // b) if isinstance(doc, int) and isinstance(query, int) else lax.div
        rem = (lambda a, b: a % b) if isinstance(doc, int) and isinstance(query, int) else lax.rem
        coords = []
        for s, m in zip(self.sizes[::-1], DOC_DIMS[::-1]):
            if m:
                coords.append(rem(doc, s))
                doc = div(doc, s)
            else:
                coords.append(rem(query, s))
                query = div(query, s)
        x, y, z = coords
        return (z * self.sizes[1] + y) * self.sizes[2] + x


def kernel(g, width, chunks, docs, acts, outg, pin, pout, starts, counts, queries, scores, grads,
           abuf, obuf, pbuf, rbuf, acc_l, acc_r, tbuf, xl, xr, lsum, gbuf, qbuf, part, sbuf,
           in_sems, own_sem, qs_sem, qr_sem, xs_sem, xr_sem, gs_sem, gr_sem, ss_sem, sr_sem):
    dp, me = lax.axis_index("dp"), lax.axis_index("tensor")
    doc, query = g.split(dp)
    nd, nq = g.nd, g.nq
    rank = pin.shape[0]
    rs = rank // width
    tok = acts.shape[0]
    k1, k2 = acts.shape[1] // chunks, outg.shape[1] // chunks
    qrows = queries.shape[0]
    drows = grads.shape[0]
    kkn = drows // docs
    nqr = qrows // kkn

    def at(dp_index, tensor_index):
        return {"dp": dp_index, "tensor": tensor_index}

    def turn(value, k, n):
        return lax.rem(value + k, n)

    def remote(src, dst, send, recv, to):
        return pltpu.make_async_remote_copy(
            src_ref=src, dst_ref=dst, send_sem=send, recv_sem=recv, device_id=to, device_id_type=MESH)

    reads = []
    for i in range(chunks):
        a, b = pl.ds(i * k1, k1), pl.ds(i * k2, k2)
        row = []
        for j, (src, dst, s) in enumerate(((pin, pbuf, a), (acts, abuf, a), (pout, rbuf, b), (outg, obuf, b))):
            copy = pltpu.make_async_copy(src.at[:, s], dst.at[:, s], in_sems.at[i, j])
            copy.start()
            row.append(copy)
        reads.append(row)

    barrier = pltpu.get_barrier_semaphore()
    q_peers = [turn(query, k, nq) for k in range(1, nq)]
    q_devs = [at(g.join(doc, p), me) for p in q_peers]
    t_peers = [turn(me, k, width) for k in range(1, width)]
    d_peers = [turn(doc, k, nd) for k in range(1, nd)]
    s_peers = [(turn(doc, kd, nd), turn(me, kc, width))
               for kd in range(nd) for kc in range(width) if kd or kc]
    greeted = q_devs + [at(g.join(d, query), c) for d, c in s_peers]
    for to in greeted:
        pl.semaphore_signal(barrier, inc=1, device_id=to, device_id_type=MESH)
    pl.semaphore_wait(barrier, len(greeted))

    mine = pl.ds(pl.multiple_of(query * qrows, 8), qrows)
    own = pltpu.make_async_copy(queries, qbuf.at[mine], own_sem)
    own.start()
    sends = []
    for k, to in enumerate(q_devs):
        copy = remote(queries, qbuf.at[mine], qs_sem.at[k], qr_sem.at[query], to)
        copy.start()
        sends.append(copy)

    for i in range(chunks):
        for copy in reads[i]:
            copy.wait()
        a, b = pl.ds(i * k1, k1), pl.ds(i * k2, k2)
        dl = lax.dot_general(abuf[:, a], pbuf[:, a], NT, preferred_element_type=jnp.float32)
        dr = lax.dot_general(obuf[:, b], rbuf[:, b], NT, preferred_element_type=jnp.float32)
        if i:
            dl, dr = dl + acc_l[...], dr + acc_r[...]
        if i < chunks - 1:
            acc_l[...] = dl
            acc_r[...] = dr
    tbuf[...] = jnp.concatenate([dl, dr], axis=1).T

    rights = pl.ds(rank, rank)
    for k, p in enumerate(t_peers):
        share = pl.ds(pl.multiple_of(p * rs, 8), rs)
        for j, (src, dst) in enumerate(((tbuf.at[rights], xr), (tbuf.at[share], xl))):
            copy = remote(src, dst.at[me], xs_sem.at[k, j], xr_sem.at[me, j], at(dp, p))
            copy.start()
            sends.append(copy)
    left = tbuf[pl.ds(pl.multiple_of(me * rs, 8), rs), :]
    right = tbuf[rights, :]
    for k, p in enumerate(t_peers):
        for j, dst in enumerate((xr, xl)):
            remote(dst.at[p], dst.at[p], xs_sem.at[k, j], xr_sem.at[p, j], at(dp, p)).wait_recv()
        left = left + xl[p]
        right = right + xr[p]
    tiles = tok // 128
    for i in range(tiles):
        lsum[i * rs:(i + 1) * rs, :] = left[:, i * 128:(i + 1) * 128]

    slot = lax.broadcasted_iota(jnp.int32, (1, tok), 1)
    count = counts[0]
    member = []
    for d in range(docs):
        end = count if d == docs - 1 else jnp.minimum(starts[d + 1], count)
        member.append(jnp.where((slot >= starts[d]) & (slot < end), 1.0, 0.0))
    halves = []
    for odd in range(2):
        rows = jnp.concatenate(
            [lsum[pl.ds(i * rs + odd, rs // 2, stride=2), :] for i in range(tiles)], axis=1)
        spread = jnp.concatenate([rows * m for m in member], axis=0)
        halves.append(lax.dot_general(spread, right, NT, precision=HIGHEST, preferred_element_type=jnp.float32))
    mine_grads = jnp.concatenate(halves, axis=1)
    grads[...] = mine_grads
    gmine = pl.ds(pl.multiple_of(doc * drows, 8), drows)
    gbuf[gmine, :] = mine_grads
    for k, d in enumerate(d_peers):
        copy = remote(gbuf.at[gmine], gbuf.at[gmine], gs_sem.at[k], gr_sem.at[doc], at(g.join(d, query), me))
        copy.start()
        sends.append(copy)

    own.wait()
    for k, p in enumerate(q_peers):
        there = qbuf.at[pl.ds(pl.multiple_of(p * qrows, 8), qrows)]
        remote(there, there, qs_sem.at[k], qr_sem.at[p], q_devs[k]).wait_recv()
    q = jnp.concatenate([qbuf[pl.ds(k, nq * nqr, stride=kkn), :] for k in range(kkn)], axis=1)
    for k, d in enumerate(d_peers):
        there = gbuf.at[pl.ds(pl.multiple_of(d * drows, 8), drows)]
        remote(there, there, gs_sem.at[k], gr_sem.at[d], at(g.join(d, query), me)).wait_recv()
    gr = jnp.concatenate([gbuf[pl.ds(k, nd * docs, stride=kkn), :] for k in range(kkn)], axis=1)
    s = lax.dot_general(gr, q, NT, precision=HIGHEST, preferred_element_type=jnp.float32)
    for d in range(nd):
        part[d] = s[d * docs:(d + 1) * docs, :]
    mine_slot = doc * width + me
    for k, (d, c) in enumerate(s_peers):
        copy = remote(part.at[d], sbuf.at[mine_slot], ss_sem.at[k], sr_sem.at[mine_slot], at(g.join(d, query), c))
        copy.start()
        sends.append(copy)
    sbuf[mine_slot] = part[doc]
    for k, (d, c) in enumerate(s_peers):
        there = sbuf.at[d * width + c]
        remote(there, there, ss_sem.at[k], sr_sem.at[d * width + c], at(g.join(d, query), c)).wait_recv()
    pieces = {}
    for d in range(nd):
        total = sbuf[d * width]
        for c in range(1, width):
            total = total + sbuf[d * width + c]
        for p in range(nq):
            pieces[g.join(d, p)] = total[:, p * nqr:(p + 1) * nqr]
    scores[...] = jnp.concatenate([pieces[i] for i in range(nd * nq)], axis=1)
    for copy in sends:
        copy.wait_send()


def shards(n_dp, width, acts, out_grads, proj_in, proj_out, doc_starts, token_counts, queries):
    layers, tok, f1 = acts.shape
    f2 = out_grads.shape[2]
    rank = proj_in.shape[2]
    docs = doc_starts.shape[0]
    nqr, _, share = queries.shape
    g = Group(n_dp)
    kkn = share // 128
    rs = rank // width
    chunks = math.gcd(f1 // 256, f2 // 256)
    lanes = 2 * rank
    f32, bf16 = jnp.float32, jnp.bfloat16
    dma = pltpu.SemaphoreType.DMA
    hbm = pl.BlockSpec(memory_space=pl.ANY)
    smem = pl.BlockSpec(memory_space=pltpu.SMEM)
    vmem = pl.BlockSpec(memory_space=pltpu.VMEM)
    scores, grads = pl.pallas_call(
        functools.partial(kernel, g, width, chunks, docs),
        out_shape=(jax.ShapeDtypeStruct((docs, nqr * n_dp), f32),
                   jax.ShapeDtypeStruct((docs * kkn, 128), f32)),
        in_specs=[hbm, hbm, hbm, hbm, smem, smem, hbm],
        out_specs=(vmem, vmem),
        scratch_shapes=[
            pltpu.VMEM((tok, f1), bf16),
            pltpu.VMEM((tok, f2), bf16),
            pltpu.VMEM((rank, f1), bf16),
            pltpu.VMEM((rank, f2), bf16),
            pltpu.VMEM((tok, rank), f32),
            pltpu.VMEM((tok, rank), f32),
            pltpu.VMEM((lanes, tok), f32),
            pltpu.VMEM((width, rs, tok), f32),
            pltpu.VMEM((width, rank, tok), f32),
            pltpu.VMEM((tok // 128 * rs, 128), f32),
            pltpu.VMEM((g.nd * docs * kkn, 128), f32),
            pltpu.VMEM((g.nq * nqr * kkn, 128), f32),
            pltpu.VMEM((g.nd, docs, g.nq * nqr), f32),
            pltpu.VMEM((g.nd * width, docs, g.nq * nqr), f32),
            dma((chunks, 4)), dma,
            dma((g.nq,)), dma((g.nq,)),
            dma((width, 2)), dma((width, 2)),
            dma((g.nd,)), dma((g.nd,)),
            dma((g.nd * width,)), dma((g.nd * width,)),
        ],
        compiler_params=pltpu.CompilerParams(
            collective_id=0, has_side_effects=True, vmem_limit_bytes=56 * 1024 * 1024),
    )(acts[0], out_grads[0], proj_in[0].T, proj_out[0].T, doc_starts, token_counts,
      queries.reshape(nqr * kkn, 128))
    return scores.T, grads.reshape(docs, 1, share)


def solution(mesh):
    in_specs = (
        P(None, "dp", "tensor"),
        P(None, "dp", "tensor"),
        P(None, "tensor", None),
        P(None, "tensor", None),
        P("dp"),
        P("dp"),
        P("dp", None, "tensor"),
    )
    out_specs = (P(None, "dp"), P("dp", None, "tensor"))
    body = functools.partial(shards, mesh.shape["dp"], mesh.shape["tensor"])
    return jax.shard_map(body, mesh=mesh, in_specs=in_specs, out_specs=out_specs, check_vma=False)
```

```python
import functools
import math

import jax
import jax.numpy as jnp
from jax import lax
from jax.experimental import pallas as pl
from jax.experimental.pallas import tpu as pltpu
from jax.sharding import PartitionSpec as P

MESH = pl.DeviceIdType.MESH
NT = (((1,), (1,)), ((), ()))
GREET_AT = 3
DOC_DIMS = (True, False, False)


class Group:
    def __init__(self, n_dp):
        plane = math.gcd(n_dp, 4)
        y = math.gcd(plane, 2)
        self.sizes = (n_dp // plane, plane // y, y)
        self.nd = math.prod(s for s, m in zip(self.sizes, DOC_DIMS) if m)
        self.nq = math.prod(s for s, m in zip(self.sizes, DOC_DIMS) if not m)

    def split(self, dp):
        z = lax.div(dp, self.sizes[1] * self.sizes[2])
        y = lax.rem(lax.div(dp, self.sizes[2]), self.sizes[1])
        x = lax.rem(dp, self.sizes[2])
        doc, query = 0, 0
        for c, s, m in zip((z, y, x), self.sizes, DOC_DIMS):
            if m:
                doc = doc * s + c
            else:
                query = query * s + c
        return doc, query

    def join(self, doc, query):
        div = (lambda a, b: a // b) if isinstance(doc, int) and isinstance(query, int) else lax.div
        rem = (lambda a, b: a % b) if isinstance(doc, int) and isinstance(query, int) else lax.rem
        coords = []
        for s, m in zip(self.sizes[::-1], DOC_DIMS[::-1]):
            if m:
                coords.append(rem(doc, s))
                doc = div(doc, s)
            else:
                coords.append(rem(query, s))
                query = div(query, s)
        x, y, z = coords
        return (z * self.sizes[1] + y) * self.sizes[2] + x


def split(value):
    high = value.astype(jnp.bfloat16)
    return high, (value - high.astype(jnp.float32)).astype(jnp.bfloat16)


def split_dot(a, b):
    def dot(x, y):
        return lax.dot_general(x, y, NT, preferred_element_type=jnp.float32)

    return dot(a[0], b[0]) + (dot(a[0], b[1]) + dot(a[1], b[0]))


def kernel(g, width, chunks, docs, acts, outg, pin, pout, starts_hbm, counts_hbm, queries, scores, grads,
           starts, counts, abuf, obuf, pbuf, rbuf, acc_l, acc_r, tbuf, xl, xr, lsum, gbuf, qbuf, qhl, part, sbuf,
           in_sems, own_sem, bound_sem, qs_sem, qr_sem, xs_sem, xr_sem, gs_sem, gr_sem, ss_sem, sr_sem):
    dp, me = lax.axis_index("dp"), lax.axis_index("tensor")
    doc, query = g.split(dp)
    nd, nq = g.nd, g.nq
    rank = pin.shape[0]
    rs = rank // width
    tok = acts.shape[0]
    k1, k2 = acts.shape[1] // chunks, outg.shape[1] // chunks
    qrows = queries.shape[0]
    drows = grads.shape[0]
    kkn = drows // docs
    nqr = qrows // kkn

    def at(dp_index, tensor_index):
        return {"dp": dp_index, "tensor": tensor_index}

    def turn(value, k, n):
        return lax.rem(value + k, n)

    def remote(src, dst, send, recv, to):
        return pltpu.make_async_remote_copy(
            src_ref=src, dst_ref=dst, send_sem=send, recv_sem=recv, device_id=to, device_id_type=MESH)

    mine = pl.ds(pl.multiple_of(query * qrows, 8), qrows)
    own = pltpu.make_async_copy(queries, qbuf.at[mine], own_sem)
    bounds = [pltpu.make_async_copy(starts_hbm, starts, bound_sem.at[0]),
              pltpu.make_async_copy(counts_hbm, counts, bound_sem.at[1])]
    reads = []
    for i in range(chunks):
        a, b = pl.ds(i * k1, k1), pl.ds(i * k2, k2)
        row = []
        for j, (src, dst, s) in enumerate(((pin, pbuf, a), (acts, abuf, a), (pout, rbuf, b), (outg, obuf, b))):
            copy = pltpu.make_async_copy(src.at[:, s], dst.at[:, s], in_sems.at[i, j])
            copy.start()
            row.append(copy)
        reads.append(row)

    barrier = pltpu.get_barrier_semaphore()
    q_peers = [turn(query, k, nq) for k in range(1, nq)]
    q_devs = [at(g.join(doc, p), me) for p in q_peers]
    t_peers = [turn(me, k, width) for k in range(1, width)]
    d_peers = [turn(doc, k, nd) for k in range(1, nd)]
    s_peers = [(turn(doc, kd, nd), turn(me, kc, width))
               for kd in range(nd) for kc in range(width) if kd or kc]
    greeted = q_devs + [at(g.join(d, query), c) for d, c in s_peers]
    for to in greeted:
        pl.semaphore_signal(barrier, inc=1, device_id=to, device_id_type=MESH)
    sends = []

    for i in range(chunks):
        if i == min(GREET_AT, chunks - 1):
            pl.semaphore_wait(barrier, len(greeted))

            own.start()
            for copy in bounds:
                copy.start()
            for k, to in enumerate(q_devs):
                copy = remote(queries, qbuf.at[mine], qs_sem.at[k], qr_sem.at[query], to)
                copy.start()
                sends.append(copy)
        for copy in reads[i]:
            copy.wait()
        a, b = pl.ds(i * k1, k1), pl.ds(i * k2, k2)
        dl = lax.dot_general(pbuf[:, a], abuf[:, a], NT, preferred_element_type=jnp.float32)
        dr = lax.dot_general(rbuf[:, b], obuf[:, b], NT, preferred_element_type=jnp.float32)
        if i:
            dl, dr = dl + acc_l[...], dr + acc_r[...]
        if i < chunks - 1:
            acc_l[...] = dl
            acc_r[...] = dr
    tbuf[:rank, :] = dl
    tbuf[rank:, :] = dr

    rights = pl.ds(rank, rank)
    for k, p in enumerate(t_peers):
        share = pl.ds(pl.multiple_of(p * rs, 8), rs)
        for j, (src, dst) in enumerate(((tbuf.at[rights], xr), (tbuf.at[share], xl))):
            copy = remote(src, dst.at[me], xs_sem.at[k, j], xr_sem.at[me, j], at(dp, p))
            copy.start()
            sends.append(copy)
    left = tbuf[pl.ds(pl.multiple_of(me * rs, 8), rs), :]
    right = tbuf[rights, :]
    for k, p in enumerate(t_peers):
        for j, dst in enumerate((xr, xl)):
            remote(dst.at[p], dst.at[p], xs_sem.at[k, j], xr_sem.at[p, j], at(dp, p)).wait_recv()
        left = left + xl[p]
        right = right + xr[p]
    tiles = tok // 128
    for i in range(tiles):
        lsum[i * rs:(i + 1) * rs, :] = left[:, i * 128:(i + 1) * 128]

    for copy in bounds:
        copy.wait()
    slot = lax.broadcasted_iota(jnp.int32, (1, tok), 1)
    count = counts[0]
    member = []
    for d in range(docs):
        end = count if d == docs - 1 else jnp.minimum(starts[d + 1], count)
        member.append(jnp.where((slot >= starts[d]) & (slot < end), 1.0, 0.0))
    halves = []
    for odd in range(2):
        rows = jnp.concatenate(
            [lsum[pl.ds(i * rs + odd, rs // 2, stride=2), :] for i in range(tiles)], axis=1)
        spread = jnp.concatenate([rows * m for m in member], axis=0)
        halves.append(spread)
    prod = split_dot(split(jnp.concatenate(halves, axis=0)), split(right))
    mine_grads = jnp.concatenate([prod[:drows], prod[drows:]], axis=1)
    grads[...] = mine_grads
    gmine = pl.ds(pl.multiple_of(doc * drows, 8), drows)
    gbuf[gmine, :] = mine_grads
    for k, d in enumerate(d_peers):
        copy = remote(gbuf.at[gmine], gbuf.at[gmine], gs_sem.at[k], gr_sem.at[doc], at(g.join(d, query), me))
        copy.start()
        sends.append(copy)

    own.wait()
    for k, p in enumerate(q_peers):
        there = qbuf.at[pl.ds(pl.multiple_of(p * qrows, 8), qrows)]
        remote(there, there, qs_sem.at[k], qr_sem.at[p], q_devs[k]).wait_recv()
    for k in range(kkn):
        high, low = split(qbuf[pl.ds(k, nq * nqr, stride=kkn), :])
        qhl[:nq * nqr, k * 128:(k + 1) * 128] = high
        qhl[nq * nqr:, k * 128:(k + 1) * 128] = low
    for k, d in enumerate(d_peers):
        there = gbuf.at[pl.ds(pl.multiple_of(d * drows, 8), drows)]
        remote(there, there, gs_sem.at[k], gr_sem.at[d], at(g.join(d, query), me)).wait_recv()
    gr = jnp.concatenate([gbuf[pl.ds(k, nd * docs, stride=kkn), :] for k in range(kkn)], axis=1)
    s = split_dot(split(gr), (qhl[:nq * nqr, :], qhl[nq * nqr:, :]))
    for d in range(nd):
        part[d] = s[d * docs:(d + 1) * docs, :]
    mine_slot = doc * width + me
    for k, (d, c) in enumerate(s_peers):
        copy = remote(part.at[d], sbuf.at[mine_slot], ss_sem.at[k], sr_sem.at[mine_slot], at(g.join(d, query), c))
        copy.start()
        sends.append(copy)
    sbuf[mine_slot] = part[doc]
    for k, (d, c) in enumerate(s_peers):
        there = sbuf.at[d * width + c]
        remote(there, there, ss_sem.at[k], sr_sem.at[d * width + c], at(g.join(d, query), c)).wait_recv()
    pieces = {}
    for d in range(nd):
        total = sbuf[d * width]
        for c in range(1, width):
            total = total + sbuf[d * width + c]
        for p in range(nq):
            pieces[g.join(d, p)] = total[:, p * nqr:(p + 1) * nqr]
    scores[...] = jnp.concatenate([pieces[i] for i in range(nd * nq)], axis=1)
    for copy in sends:
        copy.wait_send()


def finish(scores, grads, scores_out, grads_out):
    scores_out[...] = scores[...]
    grads_out[...] = grads[...]


def shards(n_dp, width, acts, out_grads, proj_in, proj_out, doc_starts, token_counts, queries):
    layers, tok, f1 = acts.shape
    f2 = out_grads.shape[2]
    rank = proj_in.shape[2]
    docs = doc_starts.shape[0]
    nqr, _, share = queries.shape
    g = Group(n_dp)
    kkn = share // 128
    rs = rank // width
    chunks = math.gcd(f1 // 256, f2 // 256)
    lanes = 2 * rank
    f32, bf16 = jnp.float32, jnp.bfloat16
    dma = pltpu.SemaphoreType.DMA
    hbm = pl.BlockSpec(memory_space=pl.ANY)
    vmem = pl.BlockSpec(memory_space=pltpu.VMEM)
    scores, grads = pl.pallas_call(
        functools.partial(kernel, g, width, chunks, docs),
        out_shape=(jax.ShapeDtypeStruct((docs, nqr * n_dp), f32),
                   jax.ShapeDtypeStruct((docs * kkn, 128), f32)),
        in_specs=[hbm] * 7,
        out_specs=(vmem, vmem),
        scratch_shapes=[
            pltpu.SMEM((docs,), jnp.int32),
            pltpu.SMEM((1,), jnp.int32),
            pltpu.VMEM((tok, f1), bf16),
            pltpu.VMEM((tok, f2), bf16),
            pltpu.VMEM((rank, f1), bf16),
            pltpu.VMEM((rank, f2), bf16),
            pltpu.VMEM((rank, tok), f32),
            pltpu.VMEM((rank, tok), f32),
            pltpu.VMEM((lanes, tok), f32),
            pltpu.VMEM((width, rs, tok), f32),
            pltpu.VMEM((width, rank, tok), f32),
            pltpu.VMEM((tok // 128 * rs, 128), f32),
            pltpu.VMEM((g.nd * docs * kkn, 128), f32),
            pltpu.VMEM((g.nq * nqr * kkn, 128), f32),
            pltpu.VMEM((2 * g.nq * nqr, share), bf16),
            pltpu.VMEM((g.nd, docs, g.nq * nqr), f32),
            pltpu.VMEM((g.nd * width, docs, g.nq * nqr), f32),
            dma((chunks, 4)), dma, dma((2,)),
            dma((g.nq,)), dma((g.nq,)),
            dma((width, 2)), dma((width, 2)),
            dma((g.nd,)), dma((g.nd,)),
            dma((g.nd * width,)), dma((g.nd * width,)),
        ],
        compiler_params=pltpu.CompilerParams(
            collective_id=0, has_side_effects=True, vmem_limit_bytes=56 * 1024 * 1024),
    )(acts[0], out_grads[0], proj_in[0].T, proj_out[0].T, doc_starts, token_counts,
      queries.reshape(nqr * kkn, 128))
    scores, grads = pl.pallas_call(
        finish,
        out_shape=(jax.ShapeDtypeStruct(scores.shape, f32), jax.ShapeDtypeStruct(grads.shape, f32)),
        in_specs=[vmem, vmem],
        out_specs=(vmem, vmem),
    )(scores, grads)
    return scores.T, grads.reshape(docs, 1, share)


def solution(mesh):
    in_specs = (
        P(None, "dp", "tensor"),
        P(None, "dp", "tensor"),
        P(None, "tensor", None),
        P(None, "tensor", None),
        P("dp"),
        P("dp"),
        P("dp", None, "tensor"),
    )
    out_specs = (P(None, "dp"), P("dp", None, "tensor"))
    body = functools.partial(shards, mesh.shape["dp"], mesh.shape["tensor"])
    return jax.shard_map(body, mesh=mesh, in_specs=in_specs, out_specs=out_specs, check_vma=False)
```

```python
import functools
import math

import jax
import jax.numpy as jnp
from jax import lax
from jax.experimental import pallas as pl
from jax.experimental.pallas import tpu as pltpu
from jax.sharding import PartitionSpec as P

MESH = pl.DeviceIdType.MESH
NT = (((1,), (1,)), ((), ()))
GREET_AT = 3
DOC_DIMS = (True, False, False)


class Group:
    def __init__(self, n_dp):
        plane = math.gcd(n_dp, 4)
        y = math.gcd(plane, 2)
        self.sizes = (n_dp // plane, plane // y, y)
        self.nd = math.prod(s for s, m in zip(self.sizes, DOC_DIMS) if m)
        self.nq = math.prod(s for s, m in zip(self.sizes, DOC_DIMS) if not m)

    def split(self, dp):
        z = lax.div(dp, self.sizes[1] * self.sizes[2])
        y = lax.rem(lax.div(dp, self.sizes[2]), self.sizes[1])
        x = lax.rem(dp, self.sizes[2])
        doc, query = 0, 0
        for c, s, m in zip((z, y, x), self.sizes, DOC_DIMS):
            if m:
                doc = doc * s + c
            else:
                query = query * s + c
        return doc, query

    def join(self, doc, query):
        div = (lambda a, b: a // b) if isinstance(doc, int) and isinstance(query, int) else lax.div
        rem = (lambda a, b: a % b) if isinstance(doc, int) and isinstance(query, int) else lax.rem
        coords = []
        for s, m in zip(self.sizes[::-1], DOC_DIMS[::-1]):
            if m:
                coords.append(rem(doc, s))
                doc = div(doc, s)
            else:
                coords.append(rem(query, s))
                query = div(query, s)
        x, y, z = coords
        return (z * self.sizes[1] + y) * self.sizes[2] + x


def far_first(place, n):
    low, high, order = 0, n - 1, []
    for _ in range(n - 1):
        down = place - low >= high - place
        order.append(jnp.where(down, low, high))
        low, high = jnp.where(down, low + 1, low), jnp.where(down, high, high - 1)
    return order


def split(value):
    high = value.astype(jnp.bfloat16)
    return high, (value - high.astype(jnp.float32)).astype(jnp.bfloat16)


def split_dot(a, b):
    def dot(x, y):
        return lax.dot_general(x, y, NT, preferred_element_type=jnp.float32)

    return dot(a[0], b[0]) + (dot(a[0], b[1]) + dot(a[1], b[0]))


def kernel(g, width, chunks, docs, acts, outg, pin, pout, starts_hbm, counts_hbm, queries, scores, grads,
           starts, counts, abuf, obuf, pbuf, rbuf, acc_l, acc_r, tbuf, xl, xr, lsum, gbuf, qbuf, qhl, part, sbuf,
           in_sems, own_sem, bound_sem, qs_sem, qr_sem, xs_sem, xr_sem, gs_sem, gr_sem, ss_sem, sr_sem):
    dp, me = lax.axis_index("dp"), lax.axis_index("tensor")
    doc, query = g.split(dp)
    nd, nq = g.nd, g.nq
    rank = pin.shape[0]
    rs = rank // width
    tok = acts.shape[0]
    k1, k2 = acts.shape[1] // chunks, outg.shape[1] // chunks
    qrows = queries.shape[0]
    drows = grads.shape[0]
    kkn = drows // docs
    nqr = qrows // kkn

    def at(dp_index, tensor_index):
        return {"dp": dp_index, "tensor": tensor_index}

    def turn(value, k, n):
        return lax.rem(value + k, n)

    def remote(src, dst, send, recv, to):
        return pltpu.make_async_remote_copy(
            src_ref=src, dst_ref=dst, send_sem=send, recv_sem=recv, device_id=to, device_id_type=MESH)

    mine = pl.ds(pl.multiple_of(query * qrows, 8), qrows)
    own = pltpu.make_async_copy(queries, qbuf.at[mine], own_sem)
    bounds = [pltpu.make_async_copy(starts_hbm, starts, bound_sem.at[0]),
              pltpu.make_async_copy(counts_hbm, counts, bound_sem.at[1])]
    reads = []
    for i in range(chunks):
        a, b = pl.ds(i * k1, k1), pl.ds(i * k2, k2)
        row = []
        for j, (src, dst, s) in enumerate(((pin, pbuf, a), (acts, abuf, a), (pout, rbuf, b), (outg, obuf, b))):
            copy = pltpu.make_async_copy(src.at[:, s], dst.at[:, s], in_sems.at[i, j])
            copy.start()
            row.append(copy)
        reads.append(row)

    barrier = pltpu.get_barrier_semaphore()
    q_peers = [turn(query, k, nq) for k in range(1, nq)]
    q_devs = [at(g.join(doc, p), me) for p in q_peers]
    t_peers = [turn(me, k, width) for k in range(1, width)]
    d_peers = far_first(doc, nd)
    s_peers = [(d, turn(me, kc, width)) for d in d_peers for kc in range(width)] + [(doc, c) for c in t_peers]
    greeted = q_devs + [at(g.join(d, query), c) for d, c in s_peers]
    for to in greeted:
        pl.semaphore_signal(barrier, inc=1, device_id=to, device_id_type=MESH)
    sends = []

    for i in range(chunks):
        if i == min(GREET_AT, chunks - 1):
            pl.semaphore_wait(barrier, len(greeted))

            own.start()
            for copy in bounds:
                copy.start()
            for k, to in enumerate(q_devs):
                copy = remote(queries, qbuf.at[mine], qs_sem.at[k], qr_sem.at[query], to)
                copy.start()
                sends.append(copy)
        for copy in reads[i]:
            copy.wait()
        a, b = pl.ds(i * k1, k1), pl.ds(i * k2, k2)
        dl = lax.dot_general(pbuf[:, a], abuf[:, a], NT, preferred_element_type=jnp.float32)
        dr = lax.dot_general(rbuf[:, b], obuf[:, b], NT, preferred_element_type=jnp.float32)
        if i:
            dl, dr = dl + acc_l[...], dr + acc_r[...]
        if i < chunks - 1:
            acc_l[...] = dl
            acc_r[...] = dr
    tbuf[:rank, :] = dl
    tbuf[rank:, :] = dr

    rights = pl.ds(rank, rank)
    for k, p in enumerate(t_peers):
        share = pl.ds(pl.multiple_of(p * rs, 8), rs)
        for j, (src, dst) in enumerate(((tbuf.at[rights], xr), (tbuf.at[share], xl))):
            copy = remote(src, dst.at[me], xs_sem.at[k, j], xr_sem.at[me, j], at(dp, p))
            copy.start()
            sends.append(copy)
    for copy in bounds:
        copy.wait()
    slot = lax.broadcasted_iota(jnp.int32, (1, tok), 1)
    count = counts[0]
    member = []
    for d in range(docs):
        end = count if d == docs - 1 else jnp.minimum(starts[d + 1], count)
        member.append(jnp.where((slot >= starts[d]) & (slot < end), 1.0, 0.0))
    left = tbuf[pl.ds(pl.multiple_of(me * rs, 8), rs), :]
    right = tbuf[rights, :]
    for k, p in enumerate(t_peers):
        for j, dst in enumerate((xr, xl)):
            remote(dst.at[p], dst.at[p], xs_sem.at[k, j], xr_sem.at[p, j], at(dp, p)).wait_recv()
        left = left + xl[p]
        right = right + xr[p]
    tiles = tok // 128
    for i in range(tiles):
        lsum[i * rs:(i + 1) * rs, :] = left[:, i * 128:(i + 1) * 128]

    halves = []
    for odd in range(2):
        rows = jnp.concatenate(
            [lsum[pl.ds(i * rs + odd, rs // 2, stride=2), :] for i in range(tiles)], axis=1)
        spread = jnp.concatenate([rows * m for m in member], axis=0)
        halves.append(spread)
    prod = split_dot(split(jnp.concatenate(halves, axis=0)), split(right))
    mine_grads = jnp.concatenate([prod[:drows], prod[drows:]], axis=1)
    grads[...] = mine_grads
    gmine = pl.ds(pl.multiple_of(doc * drows, 8), drows)
    gbuf[gmine, :] = mine_grads
    for k, d in enumerate(d_peers):
        copy = remote(gbuf.at[gmine], gbuf.at[gmine], gs_sem.at[k], gr_sem.at[doc], at(g.join(d, query), me))
        copy.start()
        sends.append(copy)

    own.wait()
    for k, p in enumerate(q_peers):
        there = qbuf.at[pl.ds(pl.multiple_of(p * qrows, 8), qrows)]
        remote(there, there, qs_sem.at[k], qr_sem.at[p], q_devs[k]).wait_recv()
    for k in range(kkn):
        high, low = split(qbuf[pl.ds(k, nq * nqr, stride=kkn), :])
        qhl[:nq * nqr, k * 128:(k + 1) * 128] = high
        qhl[nq * nqr:, k * 128:(k + 1) * 128] = low
    for k, d in enumerate(d_peers):
        there = gbuf.at[pl.ds(pl.multiple_of(d * drows, 8), drows)]
        remote(there, there, gs_sem.at[k], gr_sem.at[d], at(g.join(d, query), me)).wait_recv()
    gr = jnp.concatenate([gbuf[pl.ds(k, nd * docs, stride=kkn), :] for k in range(kkn)], axis=1)
    s = split_dot(split(gr), (qhl[:nq * nqr, :], qhl[nq * nqr:, :]))
    for d in range(nd):
        part[d] = s[d * docs:(d + 1) * docs, :]
    mine_slot = doc * width + me
    for k, (d, c) in enumerate(s_peers):
        copy = remote(part.at[d], sbuf.at[mine_slot], ss_sem.at[k], sr_sem.at[mine_slot], at(g.join(d, query), c))
        copy.start()
        sends.append(copy)
    sbuf[mine_slot] = part[doc]
    for k, (d, c) in enumerate(s_peers):
        there = sbuf.at[d * width + c]
        remote(there, there, ss_sem.at[k], sr_sem.at[d * width + c], at(g.join(d, query), c)).wait_recv()
    pieces = {}
    for d in range(nd):
        total = sbuf[d * width]
        for c in range(1, width):
            total = total + sbuf[d * width + c]
        for p in range(nq):
            pieces[g.join(d, p)] = total[:, p * nqr:(p + 1) * nqr]
    scores[...] = jnp.concatenate([pieces[i] for i in range(nd * nq)], axis=1)
    for copy in sends:
        copy.wait_send()


def shards(n_dp, width, acts, out_grads, proj_in, proj_out, doc_starts, token_counts, queries):
    layers, tok, f1 = acts.shape
    f2 = out_grads.shape[2]
    rank = proj_in.shape[2]
    docs = doc_starts.shape[0]
    nqr, _, share = queries.shape
    g = Group(n_dp)
    kkn = share // 128
    rs = rank // width
    chunks = math.gcd(f1 // 256, f2 // 256)
    lanes = 2 * rank
    f32, bf16 = jnp.float32, jnp.bfloat16
    dma = pltpu.SemaphoreType.DMA
    hbm = pl.BlockSpec(memory_space=pltpu.HBM)
    vmem = pl.BlockSpec(memory_space=pltpu.VMEM)
    scores, grads = pl.pallas_call(
        functools.partial(kernel, g, width, chunks, docs),
        out_shape=(pltpu.VMEM((docs, nqr * n_dp), f32), pltpu.VMEM((docs * kkn, 128), f32)),
        in_specs=[hbm] * 7,
        out_specs=(vmem, vmem),
        scratch_shapes=[
            pltpu.SMEM((docs,), jnp.int32),
            pltpu.SMEM((1,), jnp.int32),
            pltpu.VMEM((tok, f1), bf16),
            pltpu.VMEM((tok, f2), bf16),
            pltpu.VMEM((rank, f1), bf16),
            pltpu.VMEM((rank, f2), bf16),
            pltpu.VMEM((rank, tok), f32),
            pltpu.VMEM((rank, tok), f32),
            pltpu.VMEM((lanes, tok), f32),
            pltpu.VMEM((width, rs, tok), f32),
            pltpu.VMEM((width, rank, tok), f32),
            pltpu.VMEM((tok // 128 * rs, 128), f32),
            pltpu.VMEM((g.nd * docs * kkn, 128), f32),
            pltpu.VMEM((g.nq * nqr * kkn, 128), f32),
            pltpu.VMEM((2 * g.nq * nqr, share), bf16),
            pltpu.VMEM((g.nd, docs, g.nq * nqr), f32),
            pltpu.VMEM((g.nd * width, docs, g.nq * nqr), f32),
            dma((chunks, 4)), dma, dma((2,)),
            dma((g.nq,)), dma((g.nq,)),
            dma((width, 2)), dma((width, 2)),
            dma((g.nd,)), dma((g.nd,)),
            dma((g.nd * width,)), dma((g.nd * width,)),
        ],
        compiler_params=pltpu.CompilerParams(
            collective_id=0, has_side_effects=True, vmem_limit_bytes=56 * 1024 * 1024),
    )(acts[0], out_grads[0], proj_in[0].T, proj_out[0].T, doc_starts, token_counts,
      queries.reshape(nqr * kkn, 128))
    return scores.T, grads.reshape(docs, 1, share)


def solution(mesh):
    in_specs = (
        P(None, "dp", "tensor"),
        P(None, "dp", "tensor"),
        P(None, "tensor", None),
        P(None, "tensor", None),
        P("dp"),
        P("dp"),
        P("dp", None, "tensor"),
    )
    out_specs = (P(None, "dp"), P("dp", None, "tensor"))
    body = functools.partial(shards, mesh.shape["dp"], mesh.shape["tensor"])
    return jax.shard_map(body, mesh=mesh, in_specs=in_specs, out_specs=out_specs, check_vma=False)
```

```python
import functools
import math

import jax
import jax.numpy as jnp
from jax import lax
from jax.experimental import pallas as pl
from jax.experimental.pallas import tpu as pltpu
from jax.sharding import PartitionSpec as P

MESH = pl.DeviceIdType.MESH
NT = (((1,), (1,)), ((), ()))
GREET_AT = 2
DOC_DIMS = (True, False, False)


class Group:
    def __init__(self, n_dp):
        plane = math.gcd(n_dp, 4)
        y = math.gcd(plane, 2)
        self.sizes = (n_dp // plane, plane // y, y)
        self.nd = math.prod(s for s, m in zip(self.sizes, DOC_DIMS) if m)
        self.nq = math.prod(s for s, m in zip(self.sizes, DOC_DIMS) if not m)

    def split(self, dp):
        z = lax.div(dp, self.sizes[1] * self.sizes[2])
        y = lax.rem(lax.div(dp, self.sizes[2]), self.sizes[1])
        x = lax.rem(dp, self.sizes[2])
        doc, query = 0, 0
        for c, s, m in zip((z, y, x), self.sizes, DOC_DIMS):
            if m:
                doc = doc * s + c
            else:
                query = query * s + c
        return doc, query

    def join(self, doc, query):
        div = (lambda a, b: a // b) if isinstance(doc, int) and isinstance(query, int) else lax.div
        rem = (lambda a, b: a % b) if isinstance(doc, int) and isinstance(query, int) else lax.rem
        coords = []
        for s, m in zip(self.sizes[::-1], DOC_DIMS[::-1]):
            if m:
                coords.append(rem(doc, s))
                doc = div(doc, s)
            else:
                coords.append(rem(query, s))
                query = div(query, s)
        x, y, z = coords
        return (z * self.sizes[1] + y) * self.sizes[2] + x


def far_first(place, n):
    low, high, order = 0, n - 1, []
    for _ in range(n - 1):
        down = place - low >= high - place
        order.append(jnp.where(down, low, high))
        low, high = jnp.where(down, low + 1, low), jnp.where(down, high, high - 1)
    return order


def split(value):
    high = value.astype(jnp.bfloat16)
    return high, (value - high.astype(jnp.float32)).astype(jnp.bfloat16)


def split_dot(a, b):
    def dot(x, y):
        return lax.dot_general(x, y, NT, preferred_element_type=jnp.float32)

    return dot(a[0], b[0]) + (dot(a[0], b[1]) + dot(a[1], b[0]))


def kernel(g, width, chunks, docs, acts, outg, pin, pout, starts_hbm, counts_hbm, queries, scores, grads,
           starts, counts, abuf, obuf, pbuf, rbuf, acc_l, acc_r, tbuf, xl, xr, lsum, gbuf, qbuf, qhl, part, sbuf,
           in_sems, own_sem, bound_sem, qs_sem, qr_sem, xs_sem, xr_sem, gs_sem, gr_sem, ss_sem, sr_sem):
    dp, me = lax.axis_index("dp"), lax.axis_index("tensor")
    doc, query = g.split(dp)
    nd, nq = g.nd, g.nq
    rank = pin.shape[0]
    rs = rank // width
    tok = acts.shape[0]
    k1, k2 = acts.shape[1] // chunks, outg.shape[1] // chunks
    qrows = queries.shape[0]
    drows = grads.shape[0]
    kkn = drows // docs
    nqr = qrows // kkn

    def at(dp_index, tensor_index):
        return {"dp": dp_index, "tensor": tensor_index}

    def turn(value, k, n):
        return lax.rem(value + k, n)

    def remote(src, dst, send, recv, to):
        return pltpu.make_async_remote_copy(
            src_ref=src, dst_ref=dst, send_sem=send, recv_sem=recv, device_id=to, device_id_type=MESH)

    mine = pl.ds(pl.multiple_of(query * qrows, 8), qrows)
    own = pltpu.make_async_copy(queries, qbuf.at[mine], own_sem)
    bounds = [pltpu.make_async_copy(starts_hbm, starts, bound_sem.at[0]),
              pltpu.make_async_copy(counts_hbm, counts, bound_sem.at[1])]
    reads = []
    for i in range(chunks):
        a, b = pl.ds(i * k1, k1), pl.ds(i * k2, k2)
        row = []
        for j, (src, dst, s) in enumerate(((pin, pbuf, a), (acts, abuf, a), (pout, rbuf, b), (outg, obuf, b))):
            copy = pltpu.make_async_copy(src.at[:, s], dst.at[:, s], in_sems.at[i, j])
            copy.start()
            row.append(copy)
        reads.append(row)

    barrier = pltpu.get_barrier_semaphore()
    q_peers = [turn(query, k, nq) for k in range(1, nq)]
    q_devs = [at(g.join(doc, p), me) for p in q_peers]
    t_peers = [turn(me, k, width) for k in range(1, width)]
    d_peers = far_first(doc, nd)
    s_peers = [(d, turn(me, kc, width)) for d in d_peers for kc in range(width)] + [(doc, c) for c in t_peers]
    greeted = q_devs + [at(g.join(d, query), c) for d, c in s_peers]
    for to in greeted:
        pl.semaphore_signal(barrier, inc=1, device_id=to, device_id_type=MESH)
    sends = []

    for i in range(chunks):
        if i == min(GREET_AT, chunks - 1):
            pl.semaphore_wait(barrier, len(greeted))

            own.start()
            for copy in bounds:
                copy.start()
            for k, to in enumerate(q_devs):
                copy = remote(queries, qbuf.at[mine], qs_sem.at[k], qr_sem.at[query], to)
                copy.start()
                sends.append(copy)
        for copy in reads[i]:
            copy.wait()
        a, b = pl.ds(i * k1, k1), pl.ds(i * k2, k2)
        dl = lax.dot_general(pbuf[:, a], abuf[:, a], NT, preferred_element_type=jnp.float32)
        dr = lax.dot_general(rbuf[:, b], obuf[:, b], NT, preferred_element_type=jnp.float32)
        if i:
            dl, dr = dl + acc_l[...], dr + acc_r[...]
        if i < chunks - 1:
            acc_l[...] = dl
            acc_r[...] = dr
    tbuf[:rank, :] = dl
    tbuf[rank:, :] = dr

    rights = pl.ds(rank, rank)
    for k, p in enumerate(t_peers):
        share = pl.ds(pl.multiple_of(p * rs, 8), rs)
        for j, (src, dst) in enumerate(((tbuf.at[rights], xr), (tbuf.at[share], xl))):
            copy = remote(src, dst.at[me], xs_sem.at[k, j], xr_sem.at[me, j], at(dp, p))
            copy.start()
            sends.append(copy)
    for copy in bounds:
        copy.wait()
    slot = lax.broadcasted_iota(jnp.int32, (1, tok), 1)
    count = counts[0]
    member = []
    for d in range(docs):
        end = count if d == docs - 1 else jnp.minimum(starts[d + 1], count)
        member.append(jnp.where((slot >= starts[d]) & (slot < end), 1.0, 0.0))
    left = tbuf[pl.ds(pl.multiple_of(me * rs, 8), rs), :]
    right = tbuf[rights, :]
    for k, p in enumerate(t_peers):
        for j, dst in enumerate((xr, xl)):
            remote(dst.at[p], dst.at[p], xs_sem.at[k, j], xr_sem.at[p, j], at(dp, p)).wait_recv()
        left = left + xl[p]
        right = right + xr[p]
    tiles = tok // 128
    for i in range(tiles):
        lsum[i * rs:(i + 1) * rs, :] = left[:, i * 128:(i + 1) * 128]

    halves = []
    for odd in range(2):
        rows = jnp.concatenate(
            [lsum[pl.ds(i * rs + odd, rs // 2, stride=2), :] for i in range(tiles)], axis=1)
        spread = jnp.concatenate([rows * m for m in member], axis=0)
        halves.append(spread)
    prod = split_dot(split(jnp.concatenate(halves, axis=0)), split(right))
    mine_grads = jnp.concatenate([prod[:drows], prod[drows:]], axis=1)
    grads[...] = mine_grads
    gmine = pl.ds(pl.multiple_of(doc * drows, 8), drows)
    gbuf[gmine, :] = mine_grads
    for k, d in enumerate(d_peers):
        copy = remote(gbuf.at[gmine], gbuf.at[gmine], gs_sem.at[k], gr_sem.at[doc], at(g.join(d, query), me))
        copy.start()
        sends.append(copy)

    own.wait()
    for k, p in enumerate(q_peers):
        there = qbuf.at[pl.ds(pl.multiple_of(p * qrows, 8), qrows)]
        remote(there, there, qs_sem.at[k], qr_sem.at[p], q_devs[k]).wait_recv()
    for k in range(kkn):
        high, low = split(qbuf[pl.ds(k, nq * nqr, stride=kkn), :])
        qhl[:nq * nqr, k * 128:(k + 1) * 128] = high
        qhl[nq * nqr:, k * 128:(k + 1) * 128] = low
    for k, d in enumerate(d_peers):
        there = gbuf.at[pl.ds(pl.multiple_of(d * drows, 8), drows)]
        remote(there, there, gs_sem.at[k], gr_sem.at[d], at(g.join(d, query), me)).wait_recv()
    gr = jnp.concatenate([gbuf[pl.ds(k, nd * docs, stride=kkn), :] for k in range(kkn)], axis=1)
    s = split_dot(split(gr), (qhl[:nq * nqr, :], qhl[nq * nqr:, :]))
    for d in range(nd):
        part[d] = s[d * docs:(d + 1) * docs, :]
    mine_slot = doc * width + me
    for k, (d, c) in enumerate(s_peers):
        copy = remote(part.at[d], sbuf.at[mine_slot], ss_sem.at[k], sr_sem.at[mine_slot], at(g.join(d, query), c))
        copy.start()
        sends.append(copy)
    sbuf[mine_slot] = part[doc]
    for k, (d, c) in enumerate(s_peers):
        there = sbuf.at[d * width + c]
        remote(there, there, ss_sem.at[k], sr_sem.at[d * width + c], at(g.join(d, query), c)).wait_recv()
    pieces = {}
    for d in range(nd):
        total = sbuf[d * width]
        for c in range(1, width):
            total = total + sbuf[d * width + c]
        for p in range(nq):
            pieces[g.join(d, p)] = total[:, p * nqr:(p + 1) * nqr]
    scores[...] = jnp.concatenate([pieces[i] for i in range(nd * nq)], axis=1)
    for copy in sends:
        copy.wait_send()


def shards(n_dp, width, acts, out_grads, proj_in, proj_out, doc_starts, token_counts, queries):
    layers, tok, f1 = acts.shape
    f2 = out_grads.shape[2]
    rank = proj_in.shape[2]
    docs = doc_starts.shape[0]
    nqr, _, share = queries.shape
    g = Group(n_dp)
    kkn = share // 128
    rs = rank // width
    chunks = math.gcd(f1 // 256, f2 // 256)
    lanes = 2 * rank
    f32, bf16 = jnp.float32, jnp.bfloat16
    dma = pltpu.SemaphoreType.DMA
    hbm = pl.BlockSpec(memory_space=pltpu.HBM)
    vmem = pl.BlockSpec(memory_space=pltpu.VMEM)
    scores, grads = pl.pallas_call(
        functools.partial(kernel, g, width, chunks, docs),
        out_shape=(pltpu.VMEM((docs, nqr * n_dp), f32), pltpu.VMEM((docs * kkn, 128), f32)),
        in_specs=[hbm] * 7,
        out_specs=(vmem, vmem),
        scratch_shapes=[
            pltpu.SMEM((docs,), jnp.int32),
            pltpu.SMEM((1,), jnp.int32),
            pltpu.VMEM((tok, f1), bf16),
            pltpu.VMEM((tok, f2), bf16),
            pltpu.VMEM((rank, f1), bf16),
            pltpu.VMEM((rank, f2), bf16),
            pltpu.VMEM((rank, tok), f32),
            pltpu.VMEM((rank, tok), f32),
            pltpu.VMEM((lanes, tok), f32),
            pltpu.VMEM((width, rs, tok), f32),
            pltpu.VMEM((width, rank, tok), f32),
            pltpu.VMEM((tok // 128 * rs, 128), f32),
            pltpu.VMEM((g.nd * docs * kkn, 128), f32),
            pltpu.VMEM((g.nq * nqr * kkn, 128), f32),
            pltpu.VMEM((2 * g.nq * nqr, share), bf16),
            pltpu.VMEM((g.nd, docs, g.nq * nqr), f32),
            pltpu.VMEM((g.nd * width, docs, g.nq * nqr), f32),
            dma((chunks, 4)), dma, dma((2,)),
            dma((g.nq,)), dma((g.nq,)),
            dma((width, 2)), dma((width, 2)),
            dma((g.nd,)), dma((g.nd,)),
            dma((g.nd * width,)), dma((g.nd * width,)),
        ],
        compiler_params=pltpu.CompilerParams(
            collective_id=0, has_side_effects=True, vmem_limit_bytes=56 * 1024 * 1024),
    )(acts[0], out_grads[0], proj_in[0].T, proj_out[0].T, doc_starts, token_counts,
      queries.reshape(nqr * kkn, 128))
    return scores.T, grads.reshape(docs, 1, share)


def solution(mesh):
    in_specs = (
        P(None, "dp", "tensor"),
        P(None, "dp", "tensor"),
        P(None, "tensor", None),
        P(None, "tensor", None),
        P("dp"),
        P("dp"),
        P("dp", None, "tensor"),
    )
    out_specs = (P(None, "dp"), P("dp", None, "tensor"))
    body = functools.partial(shards, mesh.shape["dp"], mesh.shape["tensor"])
    return jax.shard_map(body, mesh=mesh, in_specs=in_specs, out_specs=out_specs, check_vma=False)
```
